128 devices in a mesh: hst: 16 (over y, x_lo, core), head: 8 (over x_hi, z).
Axes of the slice: x: 4 (x_hi: 2, x_lo: 2; x = x_hi * 2 + x_lo), y: 4, z: 4, core: 2. Of those that a mesh axis runs over, the one named last changes fastest.
Arguments:
- context_query: bfloat16 [65536, 64, 128], P('hst', 'head'), may hold values from -8 to 8
- context_key: bfloat16 [65536, 8, 128], P('hst', 'head'), may hold values from -6 to 6
- context_value: bfloat16 [65536, 8, 128], P('hst', 'head'), may hold values from -6 to 6
- question: bfloat16 [128, 8192], P('hst', 'head'), may hold values from -8 to 8
- out_weight: bfloat16 [8192, 8192], P('head', 'hst'), may hold values from -0.5 to 0.5
- block_tenant: int32 [256], P('hst'), may hold values from 0 to 7, as said below
- tenant_length: int32 [8], replicated, may hold values from 257 to 31232, as said below
- slot_tenant: int32 [8], replicated, may hold values from 0 to 7, each once
Outputs:
- context_out: bfloat16 [65536, 64, 128], P('hst', 'head')
- query_out: bfloat16 [128, 8192], P('head', 'hst')
The draws below stay inside these ranges and needn't reach their ends.
Inputs may be any that keep to these rules, and one draw needn't show every extreme that they name: `block_tenant`: every tenant owns at least two blocks; the busiest tenant owns 2 + 241 // 2 blocks and no tenant owns more. `tenant_length`: a tenant that owns c blocks has a length above (c - 1) * 256 and at most c * 256; the busiest tenant's last block is full. `slot_tenant`: each tenant stands in exactly one slot.
All inputs are finite; a program needn't handle non-finite values.
Results may differ from the reference program's by a relative error of at most 0.0052.
Values may be sent and summed in bfloat16 or wider, within the bound.
No kernel may reach another device: no remote copies, remote signals or barrier semaphores. Data moves between devices by JAX's collectives and lax.ppermute only.
A program may use at most 64 MiB of HBM per device.

```python
import jax
import jax.numpy as jnp
from jax import lax

D = 8192
QH = 64
KVH = 8
HD = 128
BS = 256
QT = 16
TEN = 8
NB = 256


def tenant_plan(key):
    spare_count = NB - 2 * TEN
    light_spare = spare_count // 2
    heavy_spare = spare_count - light_spare
    first_pick = jax.random.randint(jax.random.fold_in(key, 101), (light_spare,), 1, TEN)
    second_pick = jax.random.randint(jax.random.fold_in(key, 102), (light_spare,), 1, TEN)
    renamed = jax.random.permutation(jax.random.fold_in(key, 103), TEN).astype(jnp.int32)
    chosen = renamed[jnp.minimum(first_pick, second_pick)]
    tenant_ids = jnp.arange(TEN, dtype=jnp.int32)
    is_heavy = (tenant_ids == renamed[0]).astype(jnp.int32)
    counts = 2 + heavy_spare * is_heavy + jnp.sum((chosen[:, None] == tenant_ids[None, :]).astype(jnp.int32), axis=0)
    block_ends = jnp.cumsum(counts)
    places = jnp.arange(NB, dtype=jnp.int32)
    sorted_tenant = jnp.sum((places[:, None] >= block_ends[None, :]).astype(jnp.int32), axis=1)
    shuffle = jax.random.permutation(jax.random.fold_in(key, 104), NB)
    tail_tokens = jax.random.randint(jax.random.fold_in(key, 105), (TEN,), 1, BS + 1)
    tail_tokens = jnp.where(is_heavy > 0, BS, tail_tokens)
    return (sorted_tenant[shuffle].astype(jnp.int32), ((counts - 1) * BS + tail_tokens).astype(jnp.int32))


def draw_block_tenant(key, part):
    return tenant_plan(key)[0]


def draw_tenant_length(key, part):
    return tenant_plan(key)[1]


def draw_context_query(key, part):
    full_shape = (NB * BS, QH, HD)
    values_drawn = jnp.clip(2.0 * jax.random.normal(jax.random.fold_in(key, 201), full_shape, jnp.float32), -8.0, 8.0)
    return values_drawn.astype(jnp.bfloat16)


def draw_context_key(key, part):
    full_shape = (NB * BS, KVH, HD)
    values_drawn = jnp.clip(jax.random.normal(jax.random.fold_in(key, 401), full_shape, jnp.float32), -6.0, 6.0)
    return values_drawn.astype(jnp.bfloat16)


def draw_question(key, part):
    full_shape = (TEN * QT, QH * HD)
    values_drawn = jnp.clip(2.0 * jax.random.normal(jax.random.fold_in(key, 501), full_shape, jnp.float32), -8.0, 8.0)
    return values_drawn.astype(jnp.bfloat16)


def shard_levels(rng, extent, pieces, low, top_value):
    gain, own = 1.0, jax.random.fold_in(rng, 6)
    for axis_at, blocks in pieces:
        steps = jnp.exp(jax.random.uniform(jax.random.fold_in(own, axis_at), (blocks,), jnp.float32, low / len(pieces), top_value / len(pieces)))
        gain = gain * jnp.repeat(steps, extent[axis_at] // blocks).reshape([-1 if axis == axis_at else 1 for axis in range(len(extent))])
    return gain


def normal_values(own_key, dims, spread, limit, shards=(), kind=jnp.bfloat16):
    factor_of = shard_levels(own_key, dims, shards, -0.22, 0.18) if shards else 1.0
    values = jax.random.normal(own_key, dims, jnp.float32) * spread * factor_of
    return jnp.minimum(jnp.maximum(values, -limit), limit).astype(kind)


def setup_inputs(seed: int = 0) -> dict:
    key_of = jax.random.split(jax.random.key(seed), 9)
    return {
        "context_query": draw_context_query(jax.random.fold_in(key_of[8], 71), 0),
        "context_key": draw_context_key(jax.random.fold_in(key_of[8], 71), 0),
        "context_value": normal_values(key_of[2], (NB * BS, KVH, HD), 1.0, 6.0, ((0, 16), (1, 8))),
        "question": draw_question(jax.random.fold_in(key_of[8], 71), 0),
        "out_weight": normal_values(key_of[4], (QH * HD, D), HD ** -0.5, 0.5, ((0, 8), (1, 16))),
        "block_tenant": draw_block_tenant(jax.random.fold_in(key_of[8], 71), 0),
        "tenant_length": draw_tenant_length(jax.random.fold_in(key_of[8], 71), 0),
        "slot_tenant": jax.random.permutation(key_of[7], TEN).astype(jnp.int32),
    }


MASKED = -1e30


def rounded(values):
    return lax.optimization_barrier(values.astype(jnp.bfloat16)).astype(jnp.float32)


def reference(context_query, context_key, context_value, question, out_weight, block_tenant, tenant_length, slot_tenant):
    group_size = QH // KVH
    score_scale = HD ** -0.5
    block_order = jnp.arange(NB, dtype=jnp.int32)
    same_tenant = block_tenant[None, :] == block_tenant[:, None]
    earlier = block_order[None, :] < block_order[:, None]
    block_rank = jnp.sum((same_tenant & earlier).astype(jnp.int32), axis=1)
    leader = jnp.min(jnp.where(same_tenant, block_order[None, :], NB), axis=1).astype(jnp.int32)
    tenant_ids = jnp.arange(TEN, dtype=jnp.int32)
    tenant_hit = (block_tenant[:, None] == tenant_ids[None, :]).astype(jnp.int32)
    block_limit = jnp.sum(tenant_hit * tenant_length[None, :], axis=1)
    tenant_slot = jnp.sum(jnp.where(slot_tenant[None, :] == tenant_ids[:, None], tenant_ids[None, :], 0), axis=1)
    block_slot = jnp.sum(tenant_hit * tenant_slot[None, :], axis=1)
    query_blocks = context_query.reshape(NB, BS, KVH, group_size, HD)
    key_blocks = context_key.reshape(NB, BS, KVH, HD)
    value_blocks = context_value.reshape(NB, BS, KVH, HD)
    row_index = jnp.arange(BS, dtype=jnp.int32)
    causal = row_index[None, :] <= row_index[:, None]

    def star_block(block_index):
        query_rows = query_blocks[block_index].astype(jnp.float32)
        anchor_index = leader[block_index]
        key_rows = jnp.concatenate([key_blocks[anchor_index], key_blocks[block_index]], axis=0).astype(jnp.float32)
        value_rows = jnp.concatenate([value_blocks[anchor_index], value_blocks[block_index]], axis=0).astype(jnp.float32)
        scores = jnp.einsum("ikgd,jkd->kgij", query_rows, key_rows) * score_scale
        with_anchor = jnp.broadcast_to(block_rank[block_index] > 0, (BS, BS))
        allowed = jnp.concatenate([with_anchor, causal], axis=1)
        scores = jnp.where(allowed, scores, MASKED)
        peak_row = jnp.max(scores, axis=-1, keepdims=True)
        lifted = jnp.exp(scores - peak_row)
        totals = jnp.sum(lifted, axis=-1)
        blended = jnp.einsum("kgij,jkd->ikgd", rounded(lifted), value_rows)
        blended = blended / jnp.transpose(totals, (2, 0, 1))[..., None]
        live_rows = block_rank[block_index] * BS + row_index < block_limit[block_index]
        blended = jnp.where(live_rows[:, None, None, None], blended, 0.0)
        return blended.astype(jnp.bfloat16).reshape(BS, QH, HD)

    context_out = lax.map(star_block, block_order).reshape(NB * BS, QH, HD)

    question_rows = question.reshape(TEN, QT, KVH, group_size, HD)

    def absorb(running, block_index):
        peak_all, total_all, output_all = running
        slot_index = block_slot[block_index]
        query_rows = question_rows[slot_index].astype(jnp.float32)
        key_rows = key_blocks[block_index].astype(jnp.float32)
        value_rows = value_blocks[block_index].astype(jnp.float32)
        scores = jnp.einsum("qkgd,jkd->qkgj", query_rows, key_rows) * score_scale
        live_keys = block_rank[block_index] * BS + row_index < block_limit[block_index]
        scores = jnp.where(live_keys, scores, MASKED)
        peak_block = jnp.max(scores, axis=-1)
        lifted = jnp.exp(scores - peak_block[..., None])
        total_block = jnp.sum(lifted, axis=-1)
        part_block = jnp.einsum("qkgj,jkd->qkgd", rounded(lifted), value_rows)
        peak_old = peak_all[slot_index]
        peak_new = jnp.maximum(peak_old, peak_block)
        keep_old = jnp.exp(peak_old - peak_new)
        keep_new = jnp.exp(peak_block - peak_new)
        total_all = total_all.at[slot_index].set(total_all[slot_index] * keep_old + total_block * keep_new)
        output_all = output_all.at[slot_index].set(output_all[slot_index] * keep_old[..., None] + part_block * keep_new[..., None])
        peak_all = peak_all.at[slot_index].set(peak_new)
        return (peak_all, total_all, output_all), block_index

    start_state = (
        jnp.full((TEN, QT, KVH, group_size), MASKED, jnp.float32),
        jnp.zeros((TEN, QT, KVH, group_size), jnp.float32),
        jnp.zeros((TEN, QT, KVH, group_size, HD), jnp.float32),
    )
    final_state, visited = lax.scan(absorb, start_state, block_order)
    peak_all, total_all, output_all = final_state
    attention = (output_all / total_all[..., None]).astype(jnp.bfloat16).reshape(TEN * QT, QH * HD)
    query_out = jnp.dot(attention, out_weight, preferred_element_type=jnp.float32).astype(jnp.bfloat16)
    return context_out, query_out
```

```python
import functools

import jax
import jax.numpy as jnp
from jax import lax
from jax.experimental import pallas as pl
from jax.experimental.pallas import tpu as pltpu
from jax.sharding import PartitionSpec as P

BS = 256
QT = 16
LANES = 128
MASKED = -1e30
LOG2E = 1.4426950408889634
EXTRA = 80
PIECE = BS + EXTRA
BF = jnp.bfloat16
F32 = jnp.float32


def dot_nt(a, b):
    return lax.dot_general(a, b, (((1,), (1,)), ((), ())), preferred_element_type=F32)


def dot_nn(a, b):
    return lax.dot_general(a, b, (((1,), (0,)), ((), ())), preferred_element_type=F32)


def pack_kernel(bt_ref, key_ref, value_ref, question_ref, out_ref, first_ref, *, hosts, tenants, blocks):
    for t in range(tenants):
        first_ref[t] = 0
    for b in range(blocks - 1, -1, -1):
        first_ref[bt_ref[b]] = b
    for t in range(tenants):
        start = pl.multiple_of(first_ref[t] * BS, BS)
        out_ref[2 * t, 0:BS] = key_ref[pl.ds(start, BS), :]
        out_ref[2 * t + 1, 0:BS] = value_ref[pl.ds(start, BS), :]
    group = question_ref.shape[1] // LANES
    q = question_ref[...].astype(F32)
    for g in range(0, group, 2):
        two = jnp.concatenate([q[:, g * LANES : (g + 1) * LANES], q[:, (g + 1) * LANES : (g + 2) * LANES]], axis=0)
        two = two.astype(BF)
        for d in range(hosts):
            out_ref[d, BS + g * 8 : BS + g * 8 + 16] = two
    lane = lax.broadcasted_iota(jnp.int32, (16, LANES), 1)
    row = jnp.full((16, LANES), -1.0, F32)
    for b in range(blocks):
        row = jnp.where(lane == b, bt_ref[b].astype(F32), row)
    row = row.astype(BF)
    for d in range(hosts):
        out_ref[d, BS + 8 * group : BS + 8 * group + 16] = row


def pack(block_tenant, keys, values, question, hosts, tenants, blocks):
    return pl.pallas_call(
        functools.partial(pack_kernel, hosts=hosts, tenants=tenants, blocks=blocks),
        out_shape=jax.ShapeDtypeStruct((hosts, PIECE, LANES), BF),
        grid_spec=pltpu.PrefetchScalarGridSpec(
            num_scalar_prefetch=1,
            grid=(1,),
            in_specs=[
                pl.BlockSpec(keys.shape, lambda i, bt: (0, 0)),
                pl.BlockSpec(values.shape, lambda i, bt: (0, 0)),
                pl.BlockSpec(question.shape, lambda i, bt: (0, 0)),
            ],
            out_specs=pl.BlockSpec((hosts, PIECE, LANES), lambda i, bt: (0, 0, 0)),
            scratch_shapes=[pltpu.SMEM((tenants,), jnp.int32)],
        ),
        name="pack",
    )(block_tenant, keys, values, question)


def own_kernel(q_ref, k_ref, v_ref, o_ref, s_ref, *, heads, chunk, scale2):
    tokens = chunk
    for c in range(BS // tokens):
        t0 = c * tokens
        kmax = -(-(t0 + tokens) // LANES) * LANES
        rows = pl.ds(t0 * heads, tokens * heads)
        s = dot_nt(q_ref[rows, :], k_ref[pl.ds(0, kmax), :]).reshape(tokens, heads, kmax)
        low = kmax - LANES
        lane = lax.broadcasted_iota(jnp.int32, (tokens, heads, LANES), 2)
        tok = lax.broadcasted_iota(jnp.int32, (tokens, heads, LANES), 0) + (t0 - low)
        last = jnp.where(lane <= tok, s[:, :, low:], MASKED)
        s = last if low == 0 else jnp.concatenate([s[:, :, :low], last], axis=2)
        m = jnp.max(s, axis=2, keepdims=True) * scale2
        p = jnp.exp2(s * scale2 - m)
        v = v_ref[pl.ds(0, kmax), :]
        v = jnp.concatenate([v, jnp.ones_like(v)], axis=1)
        acc = dot_nn(p.astype(BF).reshape(tokens * heads, kmax), v)
        total = acc[:, LANES:]
        o_ref[rows, :] = (acc[:, :LANES] * (1.0 / total)).astype(o_ref.dtype)
        s_ref[rows, :] = (m + jnp.log2(total).reshape(tokens, heads, LANES)).reshape(tokens * heads, LANES)


def own_pass(query, keys, values, begin, count, heads, scale2, chunk=32, dtype=BF):
    rows = BS * heads
    return pl.pallas_call(
        functools.partial(own_kernel, heads=heads, chunk=chunk, scale2=scale2),
        out_shape=(
            jax.ShapeDtypeStruct((count * rows, LANES), dtype),
            jax.ShapeDtypeStruct((count * rows, LANES), F32),
        ),
        grid=(count,),
        in_specs=[
            pl.BlockSpec((rows, LANES), lambda b: (b + begin, 0)),
            pl.BlockSpec((BS, LANES), lambda b: (b + begin, 0)),
            pl.BlockSpec((BS, LANES), lambda b: (b + begin, 0)),
        ],
        out_specs=(
            pl.BlockSpec((rows, LANES), lambda b: (b, 0)),
            pl.BlockSpec((rows, LANES), lambda b: (b, 0)),
        ),
        cost_estimate=pl.CostEstimate(
            flops=count * rows * BS * LANES * 4 * 2, transcendentals=count * rows * BS, bytes_accessed=count * rows * LANES * 8
        ),
        name="own_pass",
    )(query, keys, values)


def anchor_kernel(meta_ref, bt_ref, q_ref, k_ref, v_ref, o_ref, s_ref, *rest, heads, chunk, scale2, begin):
    out_ref = rest[-1]
    b = pl.program_id(0) + begin
    rank = meta_ref[0, b]
    live = meta_ref[1, b]
    tokens = chunk

    @pl.when(rank == 0)
    def _():
        out_ref[...] = o_ref[...].astype(BF)

    @pl.when(rank > 0)
    def _():
        v = v_ref[...]
        v = jnp.concatenate([v, jnp.ones_like(v)], axis=1)
        for c in range(BS // tokens):
            rows = pl.ds(c * tokens * heads, tokens * heads)
            s = dot_nt(q_ref[rows, :], k_ref[...])
            lse = s_ref[rows, :]
            m = jnp.maximum(jnp.max(s, axis=1, keepdims=True) * scale2, lse)
            keep = jnp.exp2(lse - m)
            p = jnp.concatenate([jnp.exp2(s[:, :LANES] * scale2 - m), jnp.exp2(s[:, LANES:] * scale2 - m)], axis=1)
            acc = dot_nn(p.astype(BF), v)
            merged = (o_ref[rows, :].astype(F32) * keep + acc[:, :LANES]) * (1.0 / (keep + acc[:, LANES:]))
            out_ref[rows, :] = merged.astype(BF)

    @pl.when(live < BS)
    def _():
        row = lax.broadcasted_iota(jnp.int32, out_ref.shape, 0)
        out_ref[...] = jnp.where(row < live * heads, out_ref[...].astype(F32), 0.0).astype(BF)


def anchor_pass(meta, tenant, query, anchors, own, lse, begin, first, count, blocks, heads, scale2, into=None, chunk=32):
    rows = BS * heads
    in_specs = [
        pl.BlockSpec((rows, LANES), lambda b, m, t: (b + begin, 0)),
        pl.BlockSpec((None, BS, LANES), lambda b, m, t: (2 * t[b + begin], 0, 0)),
        pl.BlockSpec((None, BS, LANES), lambda b, m, t: (2 * t[b + begin] + 1, 0, 0)),
        pl.BlockSpec((rows, LANES), lambda b, m, t: (b + begin - first, 0)),
        pl.BlockSpec((rows, LANES), lambda b, m, t: (b + begin - first, 0)),
    ]
    args = [meta, tenant, query, anchors, anchors, own, lse]
    aliases = {}
    if into is not None:
        in_specs.append(pl.BlockSpec(memory_space=pl.ANY))
        args.append(into)
        aliases = {7: 0}
    return pl.pallas_call(
        functools.partial(anchor_kernel, heads=heads, chunk=chunk, scale2=scale2, begin=begin),
        out_shape=jax.ShapeDtypeStruct((blocks * rows, LANES), BF),
        grid_spec=pltpu.PrefetchScalarGridSpec(
            num_scalar_prefetch=2,
            grid=(count,),
            in_specs=in_specs,
            out_specs=pl.BlockSpec((rows, LANES), lambda b, m, t: (b + begin, 0)),
        ),
        input_output_aliases=aliases,
        cost_estimate=pl.CostEstimate(
            flops=count * rows * BS * LANES * 4 * 2, transcendentals=count * rows * BS, bytes_accessed=count * rows * LANES * 10
        ),
        name="anchor_pass",
    )(*args)


def split3(x):
    hi = x.astype(BF).astype(F32)
    mid = (x - hi).astype(BF).astype(F32)
    return hi, mid, x - hi - mid


def question_kernel(
    bt_ref, len_ref, slot_ref, me_ref, in_ref, k_ref, v_ref, out_ref, meta_ref,
    slots_of, extra, ms, ls, accs, mb, lb, ab, stage, sems, *, hosts, blocks, heads, scale2, slots,
):
    me = me_ref[0]
    half = 8 * heads
    rows = 2 * half
    fetch = pltpu.make_async_copy(in_ref.at[:, pl.ds(BS, EXTRA)], extra, sems.at[hosts])
    fetch.start()
    for s in range(slots):
        slots_of[slot_ref[s]] = s
        ms[s] = jnp.full((rows, LANES), MASKED, F32)
        ls[s] = jnp.zeros((rows, LANES), F32)
        accs[s] = jnp.zeros((rows, LANES), F32)
    fetch.wait()
    owners = jnp.concatenate([extra[h, half : half + 16, :].astype(F32)[0:1] for h in range(hosts)], axis=0)
    host = lax.broadcasted_iota(jnp.int32, (hosts, LANES), 0)
    lane = lax.broadcasted_iota(jnp.int32, (hosts, LANES), 1)
    wanted = (me // 2).astype(F32)
    source = jnp.min(jnp.where(owners == wanted, host, hosts - 1))
    load = pltpu.make_async_copy(in_ref.at[source, pl.ds(0, BS)], stage.at[pl.ds(0, BS)], sems.at[hosts])
    load.start()
    before = host * LANES + lane - me * LANES
    lives, homes = [], []
    for b in range(blocks):
        t = bt_ref[b]
        same = jnp.where((owners == t.astype(F32)) & (before < b), 1.0, 0.0)
        rank = jnp.sum(same).astype(jnp.int32)
        live = len_ref[t] - rank * BS
        meta_ref[0, b] = rank
        meta_ref[1, b] = live
        lives.append(live)
        homes.append(slots_of[t])
    for b in range(blocks):
        q = extra[pl.ds(2 * homes[b], 2), 0:half, :].reshape(rows, LANES)
        s = dot_nt(q, k_ref[pl.ds(b * BS, BS), :])
        key = lax.broadcasted_iota(jnp.int32, (rows, BS), 1)
        s = jnp.where(key < lives[b], s, MASKED)
        m = jnp.max(s, axis=1, keepdims=True) * scale2
        p = jnp.exp2(s * scale2 - m)
        v = v_ref[pl.ds(b * BS, BS), :]
        v = jnp.concatenate([v, jnp.ones_like(v)], axis=1)
        acc = dot_nn(p.astype(BF), v)
        mb[b] = jnp.broadcast_to(m, (rows, LANES))
        ab[b] = acc[:, :LANES]
        lb[b] = acc[:, LANES:]
    for b in range(blocks):
        slot = homes[b]
        m_old = ms[slot]
        m_new = jnp.maximum(m_old, mb[b])
        a = jnp.exp2(m_old - m_new)
        w = jnp.exp2(mb[b] - m_new)
        ms[slot] = m_new
        ls[slot] = ls[slot] * a + lb[b] * w
        accs[slot] = accs[slot] * a + ab[b] * w
    load.wait()
    copies = []
    for d in range(hosts):
        cp = pltpu.make_async_copy(stage.at[pl.ds(0, BS)], out_ref.at[d, pl.ds(0, BS)], sems.at[d])
        cp.start()
        copies.append(cp)
    lane1 = lax.broadcasted_iota(jnp.int32, (8, LANES), 1)
    for d in range(hosts):
        s, r0, at = d // 2, (d % 2) * half, BS + d * EXTRA
        stage[at : at + half] = accs[s, r0 : r0 + half].astype(BF)
        m_tile = jnp.zeros((8, LANES), F32)
        l_tile = jnp.zeros((8, LANES), F32)
        for g in range(heads):
            m_tile = jnp.where(lane1 % 8 == g, ms[s, r0 + 8 * g : r0 + 8 * g + 8], m_tile)
            l_tile = jnp.where(lane1 % 8 == g, ls[s, r0 + 8 * g : r0 + 8 * g + 8], l_tile)
        tile = jnp.zeros((8, LANES), F32)
        for k, piece in enumerate(split3(m_tile) + split3(l_tile)):
            tile = jnp.where(lane1 // 8 == k, piece, tile)
        tile = jnp.concatenate([tile, jnp.zeros_like(tile)], axis=0)
        stage[at + half : at + half + 16] = tile.astype(BF)
        cp = pltpu.make_async_copy(stage.at[pl.ds(at, EXTRA)], out_ref.at[d, pl.ds(BS, EXTRA)], sems.at[hosts + 1 + d])
        cp.start()
        copies.append(cp)
    for cp in copies:
        cp.wait()


def question_pass(block_tenant, tenant_length, slot_tenant, me, received, keys, values, hosts, blocks, heads, slots, scale2):
    rows = 16 * heads
    return pl.pallas_call(
        functools.partial(question_kernel, hosts=hosts, blocks=blocks, heads=heads, scale2=scale2, slots=slots),
        out_shape=(
            jax.ShapeDtypeStruct((hosts, PIECE, LANES), BF),
            jax.ShapeDtypeStruct((2, blocks), jnp.int32),
        ),
        grid_spec=pltpu.PrefetchScalarGridSpec(
            num_scalar_prefetch=4,
            grid=(1,),
            in_specs=[
                pl.BlockSpec(memory_space=pl.ANY),
                pl.BlockSpec(keys.shape, lambda i, *_: (0, 0)),
                pl.BlockSpec(values.shape, lambda i, *_: (0, 0)),
            ],
            out_specs=(pl.BlockSpec(memory_space=pl.ANY), pl.BlockSpec(memory_space=pltpu.SMEM)),
            scratch_shapes=[
                pltpu.SMEM((slots,), jnp.int32),
                pltpu.VMEM((hosts, EXTRA, LANES), BF),
                pltpu.VMEM((slots, rows, LANES), F32),
                pltpu.VMEM((slots, rows, LANES), F32),
                pltpu.VMEM((slots, rows, LANES), F32),
                pltpu.VMEM((blocks, rows, LANES), F32),
                pltpu.VMEM((blocks, rows, LANES), F32),
                pltpu.VMEM((blocks, rows, LANES), F32),
                pltpu.VMEM((BS + hosts * EXTRA, LANES), BF),
                pltpu.SemaphoreType.DMA((2 * hosts + 1,)),
            ],
        ),
        name="question_pass",
    )(block_tenant, tenant_length, slot_tenant, me, received, keys, values)


def merge_kernel(all_ref, out_ref, in_ref, sem, *, hosts, heads):
    half = 8 * heads
    fetch = pltpu.make_async_copy(all_ref.at[:, pl.ds(BS, EXTRA)], in_ref, sem)
    fetch.start()
    fetch.wait()
    stats = [in_ref[h, half : half + 16, :].astype(F32)[0:8] for h in range(hosts)]
    peaks, totals = [], []
    for x in stats:
        y = x + pltpu.roll(x, LANES - 8, 1) + pltpu.roll(x, LANES - 16, 1)
        peaks.append(y)
        totals.append(pltpu.roll(y, LANES - 24, 1))
    best = functools.reduce(jnp.maximum, peaks)
    gains = [jnp.exp2(p - best) for p in peaks]
    total = functools.reduce(jnp.add, [g * t for g, t in zip(gains, totals)])
    inverse = 1.0 / total
    gains = [g * inverse for g in gains]
    merged = []
    for g in range(heads):
        acc = jnp.zeros((8, LANES), F32)
        for h in range(hosts):
            part = in_ref[h, (g // 2) * 16 : (g // 2) * 16 + 16, :].astype(F32)[(g % 2) * 8 : (g % 2) * 8 + 8]
            acc = acc + part * jnp.broadcast_to(gains[h][:, g : g + 1], (8, LANES))
        merged.append(acc)
    for g in range(0, heads, 2):
        two = jnp.concatenate([merged[g], merged[g + 1]], axis=0).astype(BF)
        for h in range(hosts):
            out_ref[h, g * 8 : g * 8 + 16, :] = two


def merge(parts, hosts, heads):
    return pl.pallas_call(
        functools.partial(merge_kernel, hosts=hosts, heads=heads),
        out_shape=jax.ShapeDtypeStruct((hosts, 8 * heads, LANES), BF),
        in_specs=[pl.BlockSpec(memory_space=pl.ANY)],
        scratch_shapes=[pltpu.VMEM((hosts, EXTRA, LANES), BF), pltpu.SemaphoreType.DMA],
        name="merge",
    )(parts)


def project_kernel(a_ref, w_ref, out_ref, *, hosts, heads):
    acc = None
    for g in range(0, heads, 2):
        both = a_ref[:, g * 8 : g * 8 + 16, :].astype(F32)
        a = jnp.concatenate(
            [both[:, 0:8].reshape(hosts * 8, LANES), both[:, 8:16].reshape(hosts * 8, LANES)], axis=1
        ).astype(BF)
        part = dot_nn(a, w_ref[g * LANES : (g + 2) * LANES, :])
        acc = part if acc is None else acc + part
    out_ref[...] = acc.reshape(out_ref.shape)


def project(attention, weight, hosts, heads, pieces):
    rows = hosts * 8
    return pl.pallas_call(
        functools.partial(project_kernel, hosts=hosts, heads=heads),
        out_shape=jax.ShapeDtypeStruct((pieces, rows // pieces, weight.shape[1]), F32),
        name="project",
    )(attention, weight)


def sum_kernel(in_ref, out_ref):
    out_ref[...] = jnp.sum(in_ref[...], axis=0).astype(BF)


def per_device(context_query, context_key, context_value, question, out_weight, block_tenant, tenant_length, slot_tenant):
    hosts = lax.axis_size("hst")
    groups = lax.axis_size("head")
    me = lax.axis_index("hst")
    blocks = block_tenant.shape[0]
    tenants = tenant_length.shape[0]
    heads = context_query.shape[1]
    head_size = context_query.shape[2]
    scale2 = head_size ** (-0.5) * LOG2E
    query = context_query.reshape(-1, head_size)
    keys = context_key.reshape(-1, head_size)
    values = context_value.reshape(-1, head_size)

    sent = pack(block_tenant, keys, values, question, hosts, tenants, blocks)
    received = lax.all_to_all(sent, "hst", 0, 0, tiled=True)
    cut = blocks // 2
    own_a, lse_a = own_pass(query, keys, values, 0, cut, heads, scale2)
    received, own_a = lax.optimization_barrier((received, own_a))
    sent2, meta = question_pass(
        block_tenant, tenant_length, slot_tenant, me.reshape(1), received, keys, values, hosts, blocks, heads, tenants, scale2
    )
    received2 = lax.all_to_all(sent2, "hst", 0, 0, tiled=True)
    own_b, lse_b = own_pass(query, keys, values, cut, blocks - cut, heads, scale2)
    received2, own_b = lax.optimization_barrier((received2, own_b))
    sent3 = merge(received2, hosts, heads)
    received3 = lax.all_to_all(sent3, "hst", 0, 0, tiled=True)
    out_a = anchor_pass(meta, block_tenant, query, received2, own_a, lse_a, 0, 0, cut, blocks, heads, scale2)
    received3, out_a = lax.optimization_barrier((received3, out_a))
    sent4 = project(received3, out_weight, hosts, heads, groups)
    received4 = lax.all_to_all(sent4, "head", 0, 0, tiled=True)
    out = anchor_pass(meta, block_tenant, query, received2, own_b, lse_b, cut, cut, blocks - cut, blocks, heads, scale2, into=out_a)
    query_out = pl.pallas_call(
        sum_kernel, out_shape=jax.ShapeDtypeStruct(received4.shape[1:], BF), name="head_sum"
    )(received4)
    return out.reshape(context_query.shape), query_out


def solution(mesh):
    return jax.shard_map(
        per_device,
        mesh=mesh,
        in_specs=(
            P("hst", "head", None),
            P("hst", "head", None),
            P("hst", "head", None),
            P("hst", "head"),
            P("head", "hst"),
            P("hst"),
            P(),
            P(),
        ),
        out_specs=(P("hst", "head", None), P("head", "hst")),
        check_vma=False,
    )
```

```python
import functools

import jax
import jax.numpy as jnp
from jax import lax
from jax.experimental import pallas as pl
from jax.experimental.pallas import tpu as pltpu
from jax.sharding import PartitionSpec as P

BS = 256
QT = 16
LANES = 128
MASKED = -1e30
LOG2E = 1.4426950408889634
EXTRA = 80
PIECE = BS + EXTRA
HALF = BS // 2
PIECE2 = HALF + EXTRA
BF = jnp.bfloat16
F32 = jnp.float32


def dot_nt(a, b):
    return lax.dot_general(a, b, (((1,), (1,)), ((), ())), preferred_element_type=F32)


def dot_nn(a, b):
    return lax.dot_general(a, b, (((1,), (0,)), ((), ())), preferred_element_type=F32)


def split3(x):
    hi = x.astype(BF).astype(F32)
    mid = (x - hi).astype(BF).astype(F32)
    return hi, mid, x - hi - mid


def pack_kernel(bt_ref, key_ref, value_ref, question_ref, out_ref, first_ref, *, hosts, tenants, blocks):
    for t in range(tenants):
        first_ref[t] = 0
    for b in range(blocks - 1, -1, -1):
        first_ref[bt_ref[b]] = b
    for t in range(tenants):
        start = pl.multiple_of(first_ref[t] * BS, BS)
        out_ref[2 * t, 0:BS] = key_ref[pl.ds(start, BS), :]
        out_ref[2 * t + 1, 0:BS] = value_ref[pl.ds(start, BS), :]
    group = question_ref.shape[1] // LANES
    q = question_ref[...].astype(F32)
    for g in range(0, group, 2):
        two = jnp.concatenate([q[:, g * LANES : (g + 1) * LANES], q[:, (g + 1) * LANES : (g + 2) * LANES]], axis=0)
        two = two.astype(BF)
        for d in range(hosts):
            out_ref[d, BS + g * 8 : BS + g * 8 + 16] = two
    lane = lax.broadcasted_iota(jnp.int32, (16, LANES), 1)
    row = jnp.full((16, LANES), -1.0, F32)
    for b in range(blocks):
        row = jnp.where(lane == b, bt_ref[b].astype(F32), row)
    row = row.astype(BF)
    for d in range(hosts):
        out_ref[d, BS + 8 * group : BS + 8 * group + 16] = row


def pack(block_tenant, keys, values, question, hosts, tenants, blocks):
    return pl.pallas_call(
        functools.partial(pack_kernel, hosts=hosts, tenants=tenants, blocks=blocks),
        out_shape=jax.ShapeDtypeStruct((hosts, PIECE, LANES), BF),
        grid_spec=pltpu.PrefetchScalarGridSpec(
            num_scalar_prefetch=1,
            grid=(1,),
            in_specs=[
                pl.BlockSpec(keys.shape, lambda i, bt: (0, 0)),
                pl.BlockSpec(values.shape, lambda i, bt: (0, 0)),
                pl.BlockSpec(question.shape, lambda i, bt: (0, 0)),
            ],
            out_specs=pl.BlockSpec((hosts, PIECE, LANES), lambda i, bt: (0, 0, 0)),
            scratch_shapes=[pltpu.SMEM((tenants,), jnp.int32)],
        ),
        name="pack",
    )(block_tenant, keys, values, question)


def own_kernel(q_ref, k_ref, v_ref, o_ref, s_ref, *, heads, chunk, scale2):
    tokens = chunk
    for c in range(BS // tokens):
        t0 = c * tokens
        kmax = -(-(t0 + tokens) // LANES) * LANES
        rows = pl.ds(t0 * heads, tokens * heads)
        s = dot_nt(q_ref[rows, :], k_ref[pl.ds(0, kmax), :]).reshape(tokens, heads, kmax)
        low = kmax - LANES
        lane = lax.broadcasted_iota(jnp.int32, (tokens, heads, LANES), 2)
        tok = lax.broadcasted_iota(jnp.int32, (tokens, heads, LANES), 0) + (t0 - low)
        last = jnp.where(lane <= tok, s[:, :, low:], MASKED)
        s = last if low == 0 else jnp.concatenate([s[:, :, :low], last], axis=2)
        m = jnp.max(s, axis=2, keepdims=True) * scale2
        p = jnp.exp2(s * scale2 - m)
        v = v_ref[pl.ds(0, kmax), :]
        v = jnp.concatenate([v, jnp.ones_like(v)], axis=1)
        acc = dot_nn(p.astype(BF).reshape(tokens * heads, kmax), v)
        total = acc[:, LANES:]
        o_ref[rows, :] = (acc[:, :LANES] * (1.0 / total)).astype(o_ref.dtype)
        log_total = jnp.broadcast_to(m.reshape(tokens * heads, 1), total.shape) + jnp.log2(total)
        hi, mid, low3 = split3(log_total * (-1.0 / scale2))
        col = lax.broadcasted_iota(jnp.int32, total.shape, 1)
        s_ref[rows, :] = jnp.where(col == 0, hi, jnp.where(col == 1, mid, jnp.where(col == 2, low3, 0.0))).astype(BF)


def own_pass(query, keys, values, begin, count, heads, scale2, chunk=128, dtype=BF):
    rows = BS * heads
    return pl.pallas_call(
        functools.partial(own_kernel, heads=heads, chunk=chunk, scale2=scale2),
        out_shape=(
            jax.ShapeDtypeStruct((count * rows, LANES), dtype),
            jax.ShapeDtypeStruct((count * rows, LANES), BF),
        ),
        grid=(count,),
        in_specs=[
            pl.BlockSpec((rows, LANES), lambda b: (b + begin, 0)),
            pl.BlockSpec((BS, LANES), lambda b: (b + begin, 0)),
            pl.BlockSpec((BS, LANES), lambda b: (b + begin, 0)),
        ],
        out_specs=(
            pl.BlockSpec((rows, LANES), lambda b: (b, 0)),
            pl.BlockSpec((rows, LANES), lambda b: (b, 0)),
        ),
        cost_estimate=pl.CostEstimate(
            flops=count * rows * BS * LANES * 4 * 2, transcendentals=count * rows * BS, bytes_accessed=count * rows * LANES * 8
        ),
        name="own_pass",
    )(query, keys, values)


def anchor_kernel(meta_ref, bt_ref, q_ref, ka_ref, kb_ref, va_ref, vb_ref, o_ref, s_ref, *rest, heads, chunk, scale2, begin):
    out_ref = rest[-1]
    b = pl.program_id(0) + begin
    rank = meta_ref[0, b]
    live = meta_ref[1, b]
    tokens = chunk

    @pl.when(rank == 0)
    def _():
        out_ref[...] = o_ref[...].astype(BF)

    @pl.when(rank > 0)
    def _():
        v = jnp.concatenate([va_ref[...], vb_ref[...]], axis=0)
        v = jnp.concatenate([v, jnp.ones_like(v)], axis=1)
        col = lax.broadcasted_iota(jnp.int32, (BS, LANES), 1)
        k = jnp.concatenate([ka_ref[...], kb_ref[...]], axis=0)
        k = jnp.concatenate([k, jnp.where(col < 3, 1.0, 0.0).astype(BF)], axis=1)
        for c in range(BS // tokens):
            rows = pl.ds(c * tokens * heads, tokens * heads)
            s = dot_nt(jnp.concatenate([q_ref[rows, :], s_ref[rows, :]], axis=1), k)
            m = jnp.maximum(jnp.max(s, axis=1, keepdims=True), 0.0)
            keep = jnp.exp2(jnp.broadcast_to(m * -scale2, (tokens * heads, LANES)))
            p = jnp.exp2((s - m) * scale2)
            acc = dot_nn(p.astype(BF), v)
            merged = (o_ref[rows, :].astype(F32) * keep + acc[:, :LANES]) * (1.0 / (keep + acc[:, LANES:]))
            out_ref[rows, :] = merged.astype(BF)

    @pl.when(live < BS)
    def _():
        row = lax.broadcasted_iota(jnp.int32, out_ref.shape, 0)
        out_ref[...] = jnp.where(row < live * heads, out_ref[...].astype(F32), 0.0).astype(BF)


def anchor_pass(meta, tenant, query, anchors, own, lse, begin, first, count, blocks, heads, scale2, into=None, chunk=256):
    rows = BS * heads
    in_specs = [
        pl.BlockSpec((rows, LANES), lambda b, m, t: (b + begin, 0)),
        pl.BlockSpec((None, HALF, LANES), lambda b, m, t: (2 * t[b + begin], 0, 0)),
        pl.BlockSpec((None, HALF, LANES), lambda b, m, t: (2 * t[b + begin], 0, 0)),
        pl.BlockSpec((None, HALF, LANES), lambda b, m, t: (2 * t[b + begin] + 1, 0, 0)),
        pl.BlockSpec((None, HALF, LANES), lambda b, m, t: (2 * t[b + begin] + 1, 0, 0)),
        pl.BlockSpec((rows, LANES), lambda b, m, t: (b + begin - first, 0)),
        pl.BlockSpec((rows, LANES), lambda b, m, t: (b + begin - first, 0)),
    ]
    args = [meta, tenant, query, *anchors, *anchors, own, lse]
    aliases = {}
    if into is not None:
        in_specs.append(pl.BlockSpec(memory_space=pl.ANY))
        args.append(into)
        aliases = {9: 0}
    return pl.pallas_call(
        functools.partial(anchor_kernel, heads=heads, chunk=chunk, scale2=scale2, begin=begin),
        out_shape=jax.ShapeDtypeStruct((blocks * rows, LANES), BF),
        grid_spec=pltpu.PrefetchScalarGridSpec(
            num_scalar_prefetch=2,
            grid=(count,),
            in_specs=in_specs,
            out_specs=pl.BlockSpec((rows, LANES), lambda b, m, t: (b + begin, 0)),
        ),
        input_output_aliases=aliases,
        cost_estimate=pl.CostEstimate(
            flops=count * rows * BS * LANES * 4 * 2, transcendentals=count * rows * BS, bytes_accessed=count * rows * LANES * 10
        ),
        name="anchor_pass",
    )(*args)


def question_kernel(
    bt_ref, len_ref, slot_ref, me_ref, in_ref, k_hbm, v_hbm, out_ref, meta_ref,
    slots_of, k_ref, v_ref, extra, ms, ls, accs, mb, lb, ab, stage, sems, *, hosts, blocks, heads, scale2, slots,
):
    me = me_ref[0]
    half = 8 * heads
    rows = 2 * half
    fetch = pltpu.make_async_copy(in_ref.at[:, pl.ds(BS, EXTRA)], extra, sems.at[hosts])
    fetch.start()
    fetch_k = pltpu.make_async_copy(k_hbm, k_ref, sems.at[2 * hosts + 1])
    fetch_v = pltpu.make_async_copy(v_hbm, v_ref, sems.at[2 * hosts + 2])
    fetch_k.start()
    fetch_v.start()
    for s in range(slots):
        slots_of[slot_ref[s]] = s
        ms[s] = jnp.full((rows, LANES), MASKED, F32)
        ls[s] = jnp.zeros((rows, LANES), F32)
        accs[s] = jnp.zeros((rows, LANES), F32)
    fetch.wait()
    owners = jnp.concatenate([extra[h, half : half + 16, :].astype(F32)[0:1] for h in range(hosts)], axis=0)
    host = lax.broadcasted_iota(jnp.int32, (hosts, LANES), 0)
    lane = lax.broadcasted_iota(jnp.int32, (hosts, LANES), 1)
    wanted = (me // 2).astype(F32)
    source = jnp.min(jnp.where(owners == wanted, host, hosts - 1))
    load = pltpu.make_async_copy(in_ref.at[source, pl.ds(0, BS)], stage.at[pl.ds(0, BS)], sems.at[hosts])
    load.start()
    before = host * LANES + lane - me * LANES
    lives, homes = [], []
    for b in range(blocks):
        t = bt_ref[b]
        same = jnp.where((owners == t.astype(F32)) & (before < b), 1.0, 0.0)
        rank = jnp.sum(same).astype(jnp.int32)
        live = len_ref[t] - rank * BS
        meta_ref[0, b] = rank
        meta_ref[1, b] = live
        lives.append(live)
        homes.append(slots_of[t])
    load.wait()
    copies = []
    for d in range(hosts):
        cp = pltpu.make_async_copy(stage.at[pl.ds((d % 2) * HALF, HALF)], out_ref.at[d, pl.ds(0, HALF)], sems.at[d])
        cp.start()
        copies.append(cp)
    fetch_k.wait()
    fetch_v.wait()
    for b in range(blocks):
        q = extra[pl.ds(2 * homes[b], 2), 0:half, :].reshape(rows, LANES)
        s = dot_nt(q, k_ref[pl.ds(b * BS, BS), :])
        key = lax.broadcasted_iota(jnp.int32, (rows, BS), 1)
        s = jnp.where(key < lives[b], s, MASKED)
        m = jnp.max(s, axis=1, keepdims=True) * scale2
        p = jnp.exp2(s * scale2 - m)
        v = v_ref[pl.ds(b * BS, BS), :]
        v = jnp.concatenate([v, jnp.ones_like(v)], axis=1)
        acc = dot_nn(p.astype(BF), v)
        mb[b] = jnp.broadcast_to(m, (rows, LANES))
        ab[b] = acc[:, :LANES]
        lb[b] = acc[:, LANES:]
    for b in range(blocks):
        slot = homes[b]
        m_old = ms[slot]
        m_new = jnp.maximum(m_old, mb[b])
        a = jnp.exp2(m_old - m_new)
        w = jnp.exp2(mb[b] - m_new)
        ms[slot] = m_new
        ls[slot] = ls[slot] * a + lb[b] * w
        accs[slot] = accs[slot] * a + ab[b] * w
    lane1 = lax.broadcasted_iota(jnp.int32, (8, LANES), 1)
    for d in range(hosts):
        s, r0, at = d // 2, (d % 2) * half, BS + d * EXTRA
        stage[at : at + half] = accs[s, r0 : r0 + half].astype(BF)
        m_tile = jnp.zeros((8, LANES), F32)
        l_tile = jnp.zeros((8, LANES), F32)
        for g in range(heads):
            m_tile = jnp.where(lane1 % 8 == g, ms[s, r0 + 8 * g : r0 + 8 * g + 8], m_tile)
            l_tile = jnp.where(lane1 % 8 == g, ls[s, r0 + 8 * g : r0 + 8 * g + 8], l_tile)
        tile = jnp.zeros((8, LANES), F32)
        for k, piece in enumerate(split3(m_tile) + split3(l_tile)):
            tile = jnp.where(lane1 // 8 == k, piece, tile)
        tile = jnp.concatenate([tile, jnp.zeros_like(tile)], axis=0)
        stage[at + half : at + half + 16] = tile.astype(BF)
        cp = pltpu.make_async_copy(stage.at[pl.ds(at, EXTRA)], out_ref.at[d, pl.ds(HALF, EXTRA)], sems.at[hosts + 1 + d])
        cp.start()
        copies.append(cp)
    for cp in copies:
        cp.wait()


def question_pass(block_tenant, tenant_length, slot_tenant, me, received, keys, values, hosts, blocks, heads, slots, scale2):
    rows = 16 * heads
    return pl.pallas_call(
        functools.partial(question_kernel, hosts=hosts, blocks=blocks, heads=heads, scale2=scale2, slots=slots),
        out_shape=(
            jax.ShapeDtypeStruct((hosts, PIECE2, LANES), BF),
            jax.ShapeDtypeStruct((2, blocks), jnp.int32),
        ),
        grid_spec=pltpu.PrefetchScalarGridSpec(
            num_scalar_prefetch=4,
            grid=(1,),
            in_specs=[
                pl.BlockSpec(memory_space=pltpu.HBM),
                pl.BlockSpec(memory_space=pltpu.HBM),
                pl.BlockSpec(memory_space=pltpu.HBM),
            ],
            out_specs=(pl.BlockSpec(memory_space=pltpu.HBM), pl.BlockSpec(memory_space=pltpu.SMEM)),
            scratch_shapes=[
                pltpu.SMEM((slots,), jnp.int32),
                pltpu.VMEM(keys.shape, BF),
                pltpu.VMEM(values.shape, BF),
                pltpu.VMEM((hosts, EXTRA, LANES), BF),
                pltpu.VMEM((slots, rows, LANES), F32),
                pltpu.VMEM((slots, rows, LANES), F32),
                pltpu.VMEM((slots, rows, LANES), F32),
                pltpu.VMEM((blocks, rows, LANES), F32),
                pltpu.VMEM((blocks, rows, LANES), F32),
                pltpu.VMEM((blocks, rows, LANES), F32),
                pltpu.VMEM((BS + hosts * EXTRA, LANES), BF),
                pltpu.SemaphoreType.DMA((2 * hosts + 3,)),
            ],
        ),
        name="question_pass",
    )(block_tenant, tenant_length, slot_tenant, me, received, keys, values)


def merge_kernel(all_ref, out_ref, in_ref, sem, *, hosts, heads):
    half = 8 * heads
    fetch = pltpu.make_async_copy(all_ref.at[:, pl.ds(HALF, EXTRA)], in_ref, sem)
    fetch.start()
    fetch.wait()
    stats = [in_ref[h, half : half + 16, :].astype(F32)[0:8] for h in range(hosts)]
    peaks, totals = [], []
    for x in stats:
        y = x + pltpu.roll(x, LANES - 8, 1) + pltpu.roll(x, LANES - 16, 1)
        peaks.append(y)
        totals.append(pltpu.roll(y, LANES - 24, 1))
    best = functools.reduce(jnp.maximum, peaks)
    gains = [jnp.exp2(p - best) for p in peaks]
    total = functools.reduce(jnp.add, [g * t for g, t in zip(gains, totals)])
    inverse = 1.0 / total
    gains = [g * inverse for g in gains]
    merged = []
    for g in range(heads):
        acc = jnp.zeros((8, LANES), F32)
        for h in range(hosts):
            part = in_ref[h, (g // 2) * 16 : (g // 2) * 16 + 16, :].astype(F32)[(g % 2) * 8 : (g % 2) * 8 + 8]
            acc = acc + part * jnp.broadcast_to(gains[h][:, g : g + 1], (8, LANES))
        merged.append(acc)
    for g in range(0, heads, 2):
        two = jnp.concatenate([merged[g], merged[g + 1]], axis=0).astype(BF)
        for h in range(hosts):
            out_ref[h, g * 8 : g * 8 + 16, :] = two


def merge(parts, hosts, heads):
    return pl.pallas_call(
        functools.partial(merge_kernel, hosts=hosts, heads=heads),
        out_shape=jax.ShapeDtypeStruct((hosts, 8 * heads, LANES), BF),
        in_specs=[pl.BlockSpec(memory_space=pltpu.HBM)],
        scratch_shapes=[pltpu.VMEM((hosts, EXTRA, LANES), BF), pltpu.SemaphoreType.DMA],
        name="merge",
    )(parts)


def project_kernel(a_ref, w_ref, out_ref, *, hosts, heads):
    acc = None
    for g in range(0, heads, 2):
        both = a_ref[:, g * 8 : g * 8 + 16, :].astype(F32)
        a = jnp.concatenate(
            [both[:, 0:8].reshape(hosts * 8, LANES), both[:, 8:16].reshape(hosts * 8, LANES)], axis=1
        ).astype(BF)
        part = dot_nn(a, w_ref[g * LANES : (g + 2) * LANES, :])
        acc = part if acc is None else acc + part
    out_ref[...] = acc.reshape(out_ref.shape)


def project(attention, weight, hosts, heads, pieces):
    rows = hosts * 8
    return pl.pallas_call(
        functools.partial(project_kernel, hosts=hosts, heads=heads),
        out_shape=jax.ShapeDtypeStruct((pieces, rows // pieces, weight.shape[1]), F32),
        name="project",
    )(attention, weight)


def per_device(context_query, context_key, context_value, question, out_weight, block_tenant, tenant_length, slot_tenant):
    hosts = lax.axis_size("hst")
    groups = lax.axis_size("head")
    me = lax.axis_index("hst")
    blocks = block_tenant.shape[0]
    tenants = tenant_length.shape[0]
    heads = context_query.shape[1]
    head_size = context_query.shape[2]
    scale2 = head_size ** (-0.5) * LOG2E
    query = context_query.reshape(-1, head_size)
    keys = context_key.reshape(-1, head_size)
    values = context_value.reshape(-1, head_size)

    sent = pack(block_tenant, keys, values, question, hosts, tenants, blocks)
    received = lax.all_to_all(sent, "hst", 0, 0, tiled=True)
    cut = blocks * 5 // 8
    own_a, lse_a = own_pass(query, keys, values, 0, cut, heads, scale2)
    received, own_a = lax.optimization_barrier((received, own_a))
    sent2, meta = question_pass(
        block_tenant, tenant_length, slot_tenant, me.reshape(1), received, keys, values, hosts, blocks, heads, tenants, scale2
    )
    received2 = lax.all_to_all(sent2, "hst", 0, 0, tiled=True)
    own_b, lse_b = own_pass(query, keys, values, cut, blocks - cut, heads, scale2)
    received2, own_b = lax.optimization_barrier((received2, own_b))
    beside = lax.ppermute(received2, "hst", [(i, i ^ 1) for i in range(hosts)])
    anchors = (received2, beside)
    sent3 = merge(received2, hosts, heads)
    received3 = lax.all_to_all(sent3, "hst", 0, 0, tiled=True)
    out_b = anchor_pass(meta, block_tenant, query, anchors, own_b, lse_b, cut, cut, blocks - cut, blocks, heads, scale2)
    received3, out_b = lax.optimization_barrier((received3, out_b))
    sent4 = project(received3, out_weight, hosts, heads, groups)
    received4 = lax.all_to_all(sent4, "head", 0, 0, tiled=True)
    out = anchor_pass(meta, block_tenant, query, anchors, own_a, lse_a, 0, 0, cut, blocks, heads, scale2, into=out_b)
    query_out = jnp.sum(received4, axis=0).astype(BF)
    return out.reshape(context_query.shape), query_out


def solution(mesh):
    return jax.shard_map(
        per_device,
        mesh=mesh,
        in_specs=(
            P("hst", "head", None),
            P("hst", "head", None),
            P("hst", "head", None),
            P("hst", "head"),
            P("head", "hst"),
            P("hst"),
            P(),
            P(),
        ),
        out_specs=(P("hst", "head", None), P("head", "hst")),
        check_vma=False,
    )
```

```python
import functools

import jax
import jax.numpy as jnp
from jax import lax
from jax.experimental import pallas as pl
from jax.experimental.pallas import tpu as pltpu
from jax.sharding import PartitionSpec as P

BS = 256
QT = 16
LANES = 128
MASKED = -1e30
LOG2E = 1.4426950408889634
EXTRA = 80
PIECE = BS + EXTRA
HALF = BS // 2
PIECE2 = HALF + EXTRA
ROOM = (64 << 20) - (512 << 10)
GROUP = 16
BF = jnp.bfloat16
F32 = jnp.float32


def dot_nt(a, b):
    return lax.dot_general(a, b, (((1,), (1,)), ((), ())), preferred_element_type=F32)


def dot_nn(a, b):
    return lax.dot_general(a, b, (((1,), (0,)), ((), ())), preferred_element_type=F32)


def split3(x):
    hi = x.astype(BF).astype(F32)
    mid = (x - hi).astype(BF).astype(F32)
    return hi, mid, x - hi - mid


def pack_kernel(bt_ref, key_ref, value_ref, question_ref, out_ref, first_ref, *, hosts, tenants, blocks):
    for t in range(tenants):
        first_ref[t] = 0
    for b in range(blocks - 1, -1, -1):
        first_ref[bt_ref[b]] = b
    for t in range(tenants):
        start = pl.multiple_of(first_ref[t] * BS, BS)
        out_ref[2 * t, 0:BS] = key_ref[pl.ds(start, BS), :]
        out_ref[2 * t + 1, 0:BS] = value_ref[pl.ds(start, BS), :]
    group = question_ref.shape[1] // LANES
    q = question_ref[...].astype(F32)
    for g in range(0, group, 2):
        two = jnp.concatenate([q[:, g * LANES : (g + 1) * LANES], q[:, (g + 1) * LANES : (g + 2) * LANES]], axis=0)
        two = two.astype(BF)
        for d in range(hosts):
            out_ref[d, BS + g * 8 : BS + g * 8 + 16] = two
    lane = lax.broadcasted_iota(jnp.int32, (16, LANES), 1)
    row = jnp.full((16, LANES), -1.0, F32)
    for b in range(blocks):
        row = jnp.where(lane == b, bt_ref[b].astype(F32), row)
    row = row.astype(BF)
    for d in range(hosts):
        out_ref[d, BS + 8 * group : BS + 8 * group + 16] = row


def pack(block_tenant, keys, values, question, hosts, tenants, blocks):
    return pl.pallas_call(
        functools.partial(pack_kernel, hosts=hosts, tenants=tenants, blocks=blocks),
        out_shape=jax.ShapeDtypeStruct((hosts, PIECE, LANES), BF),
        grid_spec=pltpu.PrefetchScalarGridSpec(
            num_scalar_prefetch=1,
            grid=(1,),
            in_specs=[
                pl.BlockSpec(keys.shape, lambda i, bt: (0, 0)),
                pl.BlockSpec(values.shape, lambda i, bt: (0, 0)),
                pl.BlockSpec(question.shape, lambda i, bt: (0, 0)),
            ],
            out_specs=pl.BlockSpec((hosts, PIECE, LANES), lambda i, bt: (0, 0, 0)),
            scratch_shapes=[pltpu.SMEM((tenants,), jnp.int32)],
        ),
        name="pack",
    )(block_tenant, keys, values, question)


def own_kernel(q_ref, k_ref, v_ref, o_ref, s_ref, *, heads, chunk, scale2):
    tokens = chunk
    for c in range(BS // tokens):
        t0 = c * tokens
        kmax = -(-(t0 + tokens) // LANES) * LANES
        rows = pl.ds(t0 * heads, tokens * heads)
        s = dot_nt(q_ref[rows, :], k_ref[pl.ds(0, kmax), :]).reshape(tokens, heads, kmax)
        low = kmax - LANES
        lane = lax.broadcasted_iota(jnp.int32, (tokens, heads, LANES), 2)
        tok = lax.broadcasted_iota(jnp.int32, (tokens, heads, LANES), 0) + (t0 - low)
        last = jnp.where(lane <= tok, s[:, :, low:], MASKED)
        s = last if low == 0 else jnp.concatenate([s[:, :, :low], last], axis=2)
        m = jnp.max(s, axis=2, keepdims=True) * scale2
        p = jnp.exp2(s * scale2 - m)
        v = v_ref[pl.ds(0, kmax), :]
        v = jnp.concatenate([v, jnp.ones_like(v)], axis=1)
        acc = dot_nn(p.astype(BF).reshape(tokens * heads, kmax), v)
        total = acc[:, LANES:]
        o_ref[rows, :] = (acc[:, :LANES] * (1.0 / total)).astype(o_ref.dtype)
        log_total = jnp.broadcast_to(m.reshape(tokens * heads, 1), total.shape) + jnp.log2(total)
        hi, mid, low3 = split3(log_total * (-1.0 / scale2))
        lane1 = lax.broadcasted_iota(jnp.int32, (heads, LANES), 1)
        for g in range(0, tokens, GROUP):
            tile = jnp.zeros((heads, LANES), F32)
            for j in range(GROUP):
                r = slice((g + j) * heads, (g + j + 1) * heads)
                three = jnp.where(lane1 % 3 == 0, hi[r], jnp.where(lane1 % 3 == 1, mid[r], low3[r]))
                tile = jnp.where(lane1 // 3 == j, three, tile)
            at = (t0 + g) // GROUP * heads
            s_ref[at : at + heads, :] = tile


def own_pass(query, keys, values, begin, count, heads, scale2, chunk=128, dtype=BF):
    rows = BS * heads
    return pl.pallas_call(
        functools.partial(own_kernel, heads=heads, chunk=chunk, scale2=scale2),
        out_shape=(
            jax.ShapeDtypeStruct((count * rows, LANES), dtype),
            jax.ShapeDtypeStruct((count * rows // GROUP, LANES), F32),
        ),
        grid=(count,),
        in_specs=[
            pl.BlockSpec((rows, LANES), lambda b: (b + begin, 0)),
            pl.BlockSpec((BS, LANES), lambda b: (b + begin, 0)),
            pl.BlockSpec((BS, LANES), lambda b: (b + begin, 0)),
        ],
        out_specs=(
            pl.BlockSpec((rows, LANES), lambda b: (b, 0)),
            pl.BlockSpec((rows // GROUP, LANES), lambda b: (b, 0)),
        ),
        cost_estimate=pl.CostEstimate(
            flops=count * rows * BS * LANES * 4 * 2, transcendentals=count * rows * BS, bytes_accessed=count * rows * LANES * 8
        ),
        name="own_pass",
    )(query, keys, values)


def anchor_kernel(meta_ref, bt_ref, q_ref, ka_ref, kb_ref, va_ref, vb_ref, o_ref, s_ref, *rest, heads, chunk, scale2, begin):
    out_ref = rest[-1]
    b = pl.program_id(0) + begin
    rank = meta_ref[0, b]
    live = meta_ref[1, b]
    tokens = chunk

    @pl.when(rank == 0)
    def _():
        out_ref[...] = o_ref[...].astype(BF)

    @pl.when(rank > 0)
    def _():
        v = jnp.concatenate([va_ref[...], vb_ref[...]], axis=0)
        v = jnp.concatenate([v, jnp.ones_like(v)], axis=1)
        col = lax.broadcasted_iota(jnp.int32, (BS, LANES), 1)
        k = jnp.concatenate([ka_ref[...], kb_ref[...]], axis=0)
        k = jnp.concatenate([k, jnp.where(col < 3 * GROUP, 1.0, 0.0).astype(BF)], axis=1)
        lane1 = lax.broadcasted_iota(jnp.int32, (heads, LANES), 1)
        for c in range(BS // tokens):
            rows = pl.ds(c * tokens * heads, tokens * heads)
            sums = []
            for t in range(c * tokens, (c + 1) * tokens):
                at = t // GROUP * heads
                sums.append(jnp.where(lane1 // 3 == t % GROUP, s_ref[at : at + heads, :], 0.0))
            s = dot_nt(jnp.concatenate([q_ref[rows, :], jnp.concatenate(sums, axis=0).astype(BF)], axis=1), k)
            m = jnp.maximum(jnp.max(s, axis=1, keepdims=True), 0.0)
            keep = jnp.exp2(jnp.broadcast_to(m * -scale2, (tokens * heads, LANES)))
            p = jnp.exp2((s - m) * scale2)
            acc = dot_nn(p.astype(BF), v)
            merged = (o_ref[rows, :].astype(F32) * keep + acc[:, :LANES]) * (1.0 / (keep + acc[:, LANES:]))
            out_ref[rows, :] = merged.astype(BF)

    @pl.when(live < BS)
    def _():
        row = lax.broadcasted_iota(jnp.int32, out_ref.shape, 0)
        out_ref[...] = jnp.where(row < live * heads, out_ref[...].astype(F32), 0.0).astype(BF)


def anchor_pass(meta, tenant, query, anchors, own, lse, begin, first, count, blocks, heads, scale2, into=None, chunk=256):
    rows = BS * heads
    in_specs = [
        pl.BlockSpec((rows, LANES), lambda b, m, t: (b + begin, 0)),
        pl.BlockSpec((None, HALF, LANES), lambda b, m, t: (2 * t[b + begin], 0, 0)),
        pl.BlockSpec((None, HALF, LANES), lambda b, m, t: (2 * t[b + begin], 0, 0)),
        pl.BlockSpec((None, HALF, LANES), lambda b, m, t: (2 * t[b + begin] + 1, 0, 0)),
        pl.BlockSpec((None, HALF, LANES), lambda b, m, t: (2 * t[b + begin] + 1, 0, 0)),
        pl.BlockSpec((rows, LANES), lambda b, m, t: (b + begin - first, 0)),
        pl.BlockSpec((rows // GROUP, LANES), lambda b, m, t: (b + begin - first, 0)),
    ]
    args = [meta, tenant, query, *anchors, *anchors, own, lse]
    aliases = {}
    if into is not None:
        in_specs.append(pl.BlockSpec(memory_space=pl.ANY))
        args.append(into)
        aliases = {9: 0}
    return pl.pallas_call(
        functools.partial(anchor_kernel, heads=heads, chunk=chunk, scale2=scale2, begin=begin),
        out_shape=jax.ShapeDtypeStruct((blocks * rows, LANES), BF),
        grid_spec=pltpu.PrefetchScalarGridSpec(
            num_scalar_prefetch=2,
            grid=(count,),
            in_specs=in_specs,
            out_specs=pl.BlockSpec((rows, LANES), lambda b, m, t: (b + begin, 0)),
        ),
        input_output_aliases=aliases,
        cost_estimate=pl.CostEstimate(
            flops=count * rows * BS * LANES * 4 * 2, transcendentals=count * rows * BS, bytes_accessed=count * rows * LANES * 10
        ),
        name="anchor_pass",
        compiler_params=pltpu.CompilerParams(vmem_limit_bytes=ROOM),
    )(*args)


def question_kernel(
    bt_ref, len_ref, slot_ref, me_ref, in_ref, k_hbm, v_hbm, out_ref, meta_ref,
    slots_of, k_ref, v_ref, extra, ms, ls, accs, mb, lb, ab, stage, sems, *, hosts, blocks, heads, scale2, slots,
):
    me = me_ref[0]
    half = 8 * heads
    rows = 2 * half
    fetch = pltpu.make_async_copy(in_ref.at[:, pl.ds(BS, EXTRA)], extra, sems.at[hosts])
    fetch.start()
    fetch_k = pltpu.make_async_copy(k_hbm, k_ref, sems.at[2 * hosts + 1])
    fetch_v = pltpu.make_async_copy(v_hbm, v_ref, sems.at[2 * hosts + 2])
    fetch_k.start()
    fetch_v.start()
    for s in range(slots):
        slots_of[slot_ref[s]] = s
        ms[s] = jnp.full((rows, LANES), MASKED, F32)
        ls[s] = jnp.zeros((rows, LANES), F32)
        accs[s] = jnp.zeros((rows, LANES), F32)
    fetch.wait()
    owners = jnp.concatenate([extra[h, half : half + 16, :].astype(F32)[0:1] for h in range(hosts)], axis=0)
    host = lax.broadcasted_iota(jnp.int32, (hosts, LANES), 0)
    lane = lax.broadcasted_iota(jnp.int32, (hosts, LANES), 1)
    wanted = (me // 2).astype(F32)
    source = jnp.min(jnp.where(owners == wanted, host, hosts - 1))
    load = pltpu.make_async_copy(in_ref.at[source, pl.ds(0, BS)], stage.at[pl.ds(0, BS)], sems.at[hosts])
    load.start()
    before = host * LANES + lane - me * LANES
    lives, homes = [], []
    for b in range(blocks):
        t = bt_ref[b]
        same = jnp.where((owners == t.astype(F32)) & (before < b), 1.0, 0.0)
        rank = jnp.sum(same).astype(jnp.int32)
        live = len_ref[t] - rank * BS
        meta_ref[0, b] = rank
        meta_ref[1, b] = live
        lives.append(live)
        homes.append(slots_of[t])
    load.wait()
    copies = []
    for d in range(hosts):
        cp = pltpu.make_async_copy(stage.at[pl.ds((d % 2) * HALF, HALF)], out_ref.at[d, pl.ds(0, HALF)], sems.at[d])
        cp.start()
        copies.append(cp)
    fetch_k.wait()
    fetch_v.wait()
    for b in range(blocks):
        q = extra[pl.ds(2 * homes[b], 2), 0:half, :].reshape(rows, LANES)
        s = dot_nt(q, k_ref[pl.ds(b * BS, BS), :])
        key = lax.broadcasted_iota(jnp.int32, (rows, BS), 1)
        s = jnp.where(key < lives[b], s, MASKED)
        m = jnp.max(s, axis=1, keepdims=True) * scale2
        p = jnp.exp2(s * scale2 - m)
        v = v_ref[pl.ds(b * BS, BS), :]
        v = jnp.concatenate([v, jnp.ones_like(v)], axis=1)
        acc = dot_nn(p.astype(BF), v)
        mb[b] = jnp.broadcast_to(m, (rows, LANES))
        ab[b] = acc[:, :LANES]
        lb[b] = acc[:, LANES:]
    for b in range(blocks):
        slot = homes[b]
        m_old = ms[slot]
        m_new = jnp.maximum(m_old, mb[b])
        a = jnp.exp2(m_old - m_new)
        w = jnp.exp2(mb[b] - m_new)
        ms[slot] = m_new
        ls[slot] = ls[slot] * a + lb[b] * w
        accs[slot] = accs[slot] * a + ab[b] * w
    lane1 = lax.broadcasted_iota(jnp.int32, (8, LANES), 1)
    for d in range(hosts):
        s, r0, at = d // 2, (d % 2) * half, BS + d * EXTRA
        stage[at : at + half] = accs[s, r0 : r0 + half].astype(BF)
        m_tile = jnp.zeros((8, LANES), F32)
        l_tile = jnp.zeros((8, LANES), F32)
        for g in range(heads):
            m_tile = jnp.where(lane1 % 8 == g, ms[s, r0 + 8 * g : r0 + 8 * g + 8], m_tile)
            l_tile = jnp.where(lane1 % 8 == g, ls[s, r0 + 8 * g : r0 + 8 * g + 8], l_tile)
        tile = jnp.zeros((8, LANES), F32)
        for k, piece in enumerate(split3(m_tile) + split3(l_tile)):
            tile = jnp.where(lane1 // 8 == k, piece, tile)
        tile = jnp.concatenate([tile, jnp.zeros_like(tile)], axis=0)
        stage[at + half : at + half + 16] = tile.astype(BF)
        cp = pltpu.make_async_copy(stage.at[pl.ds(at, EXTRA)], out_ref.at[d, pl.ds(HALF, EXTRA)], sems.at[hosts + 1 + d])
        cp.start()
        copies.append(cp)
    for cp in copies:
        cp.wait()


def question_pass(block_tenant, tenant_length, slot_tenant, me, received, keys, values, hosts, blocks, heads, slots, scale2):
    rows = 16 * heads
    return pl.pallas_call(
        functools.partial(question_kernel, hosts=hosts, blocks=blocks, heads=heads, scale2=scale2, slots=slots),
        out_shape=(
            jax.ShapeDtypeStruct((hosts, PIECE2, LANES), BF),
            jax.ShapeDtypeStruct((2, blocks), jnp.int32),
        ),
        grid_spec=pltpu.PrefetchScalarGridSpec(
            num_scalar_prefetch=4,
            grid=(1,),
            in_specs=[
                pl.BlockSpec(memory_space=pltpu.HBM),
                pl.BlockSpec(memory_space=pltpu.HBM),
                pl.BlockSpec(memory_space=pltpu.HBM),
            ],
            out_specs=(pl.BlockSpec(memory_space=pltpu.HBM), pl.BlockSpec(memory_space=pltpu.SMEM)),
            scratch_shapes=[
                pltpu.SMEM((slots,), jnp.int32),
                pltpu.VMEM(keys.shape, BF),
                pltpu.VMEM(values.shape, BF),
                pltpu.VMEM((hosts, EXTRA, LANES), BF),
                pltpu.VMEM((slots, rows, LANES), F32),
                pltpu.VMEM((slots, rows, LANES), F32),
                pltpu.VMEM((slots, rows, LANES), F32),
                pltpu.VMEM((blocks, rows, LANES), F32),
                pltpu.VMEM((blocks, rows, LANES), F32),
                pltpu.VMEM((blocks, rows, LANES), F32),
                pltpu.VMEM((BS + hosts * EXTRA, LANES), BF),
                pltpu.SemaphoreType.DMA((2 * hosts + 3,)),
            ],
        ),
        name="question_pass",
        compiler_params=pltpu.CompilerParams(vmem_limit_bytes=ROOM),
    )(block_tenant, tenant_length, slot_tenant, me, received, keys, values)


def merge_kernel(all_ref, out_ref, in_ref, sem, *, hosts, heads):
    half = 8 * heads
    fetch = pltpu.make_async_copy(all_ref.at[:, pl.ds(HALF, EXTRA)], in_ref, sem)
    fetch.start()
    fetch.wait()
    stats = [in_ref[h, half : half + 16, :].astype(F32)[0:8] for h in range(hosts)]
    peaks, totals = [], []
    for x in stats:
        y = x + pltpu.roll(x, LANES - 8, 1) + pltpu.roll(x, LANES - 16, 1)
        peaks.append(y)
        totals.append(pltpu.roll(y, LANES - 24, 1))
    best = functools.reduce(jnp.maximum, peaks)
    gains = [jnp.exp2(p - best) for p in peaks]
    total = functools.reduce(jnp.add, [g * t for g, t in zip(gains, totals)])
    inverse = 1.0 / total
    gains = [g * inverse for g in gains]
    merged = []
    for g in range(heads):
        acc = jnp.zeros((8, LANES), F32)
        for h in range(hosts):
            part = in_ref[h, (g // 2) * 16 : (g // 2) * 16 + 16, :].astype(F32)[(g % 2) * 8 : (g % 2) * 8 + 8]
            acc = acc + part * jnp.broadcast_to(gains[h][:, g : g + 1], (8, LANES))
        merged.append(acc)
    for g in range(0, heads, 2):
        two = jnp.concatenate([merged[g], merged[g + 1]], axis=0).astype(BF)
        for h in range(hosts):
            out_ref[h, g * 8 : g * 8 + 16, :] = two


def merge(parts, hosts, heads):
    return pl.pallas_call(
        functools.partial(merge_kernel, hosts=hosts, heads=heads),
        out_shape=jax.ShapeDtypeStruct((hosts, 8 * heads, LANES), BF),
        in_specs=[pl.BlockSpec(memory_space=pltpu.HBM)],
        scratch_shapes=[pltpu.VMEM((hosts, EXTRA, LANES), BF), pltpu.SemaphoreType.DMA],
        name="merge",
        compiler_params=pltpu.CompilerParams(vmem_limit_bytes=ROOM),
    )(parts)


def project_kernel(a_ref, w_ref, out_ref, *, hosts, heads):
    acc = None
    for g in range(0, heads, 2):
        both = a_ref[:, g * 8 : g * 8 + 16, :].astype(F32)
        a = jnp.concatenate(
            [both[:, 0:8].reshape(hosts * 8, LANES), both[:, 8:16].reshape(hosts * 8, LANES)], axis=1
        ).astype(BF)
        part = dot_nn(a, w_ref[g * LANES : (g + 2) * LANES, :])
        acc = part if acc is None else acc + part
    out_ref[...] = acc.reshape(out_ref.shape)


def project(attention, weight, hosts, heads, pieces):
    rows = hosts * 8
    return pl.pallas_call(
        functools.partial(project_kernel, hosts=hosts, heads=heads),
        out_shape=jax.ShapeDtypeStruct((pieces, rows // pieces, weight.shape[1]), F32),
        name="project",
    )(attention, weight)


def per_device(context_query, context_key, context_value, question, out_weight, block_tenant, tenant_length, slot_tenant):
    hosts = lax.axis_size("hst")
    groups = lax.axis_size("head")
    me = lax.axis_index("hst")
    blocks = block_tenant.shape[0]
    tenants = tenant_length.shape[0]
    heads = context_query.shape[1]
    head_size = context_query.shape[2]
    scale2 = head_size ** (-0.5) * LOG2E
    query = context_query.reshape(-1, head_size)
    keys = context_key.reshape(-1, head_size)
    values = context_value.reshape(-1, head_size)

    sent = pack(block_tenant, keys, values, question, hosts, tenants, blocks)
    received = lax.all_to_all(sent, "hst", 0, 0, tiled=True)
    cut = blocks * 5 // 8
    own_a, lse_a = own_pass(query, keys, values, 0, cut, heads, scale2)
    received, own_a = lax.optimization_barrier((received, own_a))
    sent2, meta = question_pass(
        block_tenant, tenant_length, slot_tenant, me.reshape(1), received, keys, values, hosts, blocks, heads, tenants, scale2
    )
    received2 = lax.all_to_all(sent2, "hst", 0, 0, tiled=True)
    own_b, lse_b = own_pass(query, keys, values, cut, blocks - cut, heads, scale2)
    received2, own_b = lax.optimization_barrier((received2, own_b))
    beside = lax.ppermute(received2, "hst", [(i, i ^ 1) for i in range(hosts)])
    anchors = (received2, beside)
    sent3 = merge(received2, hosts, heads)
    received3 = lax.all_to_all(sent3, "hst", 0, 0, tiled=True)
    out_b = anchor_pass(meta, block_tenant, query, anchors, own_b, lse_b, cut, cut, blocks - cut, blocks, heads, scale2)
    received3, out_b = lax.optimization_barrier((received3, out_b))
    sent4 = project(received3, out_weight, hosts, heads, groups)
    received4 = lax.all_to_all(sent4, "head", 0, 0, tiled=True)
    out = anchor_pass(meta, block_tenant, query, anchors, own_a, lse_a, 0, 0, cut, blocks, heads, scale2, into=out_b)
    query_out = jnp.sum(received4, axis=0).astype(BF)
    return out.reshape(context_query.shape), query_out


def solution(mesh):
    return jax.shard_map(
        per_device,
        mesh=mesh,
        in_specs=(
            P("hst", "head", None),
            P("hst", "head", None),
            P("hst", "head", None),
            P("hst", "head"),
            P("head", "hst"),
            P("hst"),
            P(),
            P(),
        ),
        out_specs=(P("hst", "head", None), P("head", "hst")),
        check_vma=False,
    )
```
